32 devices in a mesh: depth: 4 (over z), height: 8 (over y, x, core).
Axes of the slice: x: 2, y: 2, z: 4, core: 2. Of those that a mesh axis runs over, the one named last changes fastest.
Arguments:
- density: float32 [32, 512, 128], P('depth', 'height'), may hold values from -6 to 6
- light_vector: float32 [3], replicated, may hold values from -1 to 1
- colour_gain: float32 [3], replicated, may hold values from 0.5 to 3
- colour_bias: float32 [3], replicated, may hold values from -1 to 1
- shear_step: int32 [4], replicated, may hold values from 0 to 32
- reverse_view: int32 [4], replicated, may hold values from 0 to 1
Outputs:
- images: float32 [4, 4, 512, 128], P(None, None, ('height', 'depth'))
The draws below stay inside these ranges and needn't reach their ends.
All inputs are finite; a program needn't handle non-finite values.
Results may differ from the reference program's by a relative error of at most 0.0003.
Values sent between devices are 32-bit elements; how exact they have to be, the bound alone decides.
A program may use at most 64 MiB of HBM per device.

```python
import jax
import jax.numpy as jnp
from jax import lax

NX = 128
VIEWS = 4
SHEAR_MAX = 32
NZ = 32
NY = 512


def place_ends(result, key, least, largest):
    place = [jax.random.randint(jax.random.fold_in(key, axis), (), 0, length) for axis, length in enumerate(result.shape)]
    widest = result.shape.index(max(result.shape))
    beside = place[:widest] + [(place[widest] + 1) % result.shape[widest]] + place[widest + 1:]
    return result.at[tuple(place)].set(least).at[tuple(beside)].set(largest)


def block_scale(key, shape, cuts, least, high):
    gain, own = 1.0, jax.random.fold_in(key, 6)
    for axis_at, parts in cuts:
        steps = jnp.exp(jax.random.uniform(jax.random.fold_in(own, axis_at), (parts,), jnp.float32, least / len(cuts), high / len(cuts)))
        gain = gain * jnp.repeat(steps, shape[axis_at] // parts).reshape([-1 if axis == axis_at else 1 for axis in range(len(shape))])
    return gain


def noise(key, shape, scale, limit, shards=(), kind=jnp.bfloat16):
    entries = jax.random.normal(key, shape, jnp.float32) * scale
    if len(shards) > 0:
        entries = block_scale(key, shape, shards, -0.22, 0.18) * entries
    return jnp.clip(entries, min=-limit, max=limit).astype(kind)


def setup_inputs(seed: int = 0) -> dict:
    key_of = jax.random.split(jax.random.key(seed), 7)
    density = noise(key_of[0], (NZ, NY, NX), 1.0, 6.0, ((0, 4), (1, 8)), jnp.float32)
    light_vector = jnp.clip(jax.random.uniform(key_of[1], (3,), jnp.float32, -1.0, 1.0), -1.0, 1.0)
    colour_gain = jnp.clip(jax.random.uniform(key_of[2], (3,), jnp.float32, 0.5, 3.0), 0.5, 3.0)
    colour_bias = jnp.clip(jax.random.uniform(key_of[3], (3,), jnp.float32, -1.0, 1.0), -1.0, 1.0)
    shear_step = place_ends(jax.random.randint(key_of[4], (VIEWS,), 0, SHEAR_MAX + 1), jax.random.fold_in(key_of[4], 1), 0, SHEAR_MAX).astype(jnp.int32)
    reverse_view = place_ends(jax.random.randint(key_of[5], (VIEWS,), 0, 2), jax.random.fold_in(key_of[5], 1), 0, 1).astype(jnp.int32)
    return {"density": density, "light_vector": light_vector, "colour_gain": colour_gain, "colour_bias": colour_bias, "shear_step": shear_step, "reverse_view": reverse_view}


EXTINCTION = 2.5

def shade_block(padded, light_vector, colour_gain, colour_bias, extinction):
    centre = padded[1:-1, 1:-1, 1:-1]
    tilt_depth = 0.5 * (padded[2:, 1:-1, 1:-1] - padded[:-2, 1:-1, 1:-1])
    tilt_rows = 0.5 * (padded[1:-1, 2:, 1:-1] - padded[1:-1, :-2, 1:-1])
    tilt_cols = 0.5 * (padded[1:-1, 1:-1, 2:] - padded[1:-1, 1:-1, :-2])
    facing = (light_vector[0] * tilt_depth + light_vector[1] * tilt_rows + light_vector[2] * tilt_cols) * lax.rsqrt(1.0 + tilt_depth * tilt_depth + tilt_rows * tilt_rows + tilt_cols * tilt_cols)
    shading = 0.25 + 1.5 * jnp.maximum(facing, 0.0)
    optical = extinction * jax.nn.softplus(centre)
    opacity = -jnp.expm1(-optical)
    colour = jax.nn.sigmoid(colour_gain[:, None, None, None] * centre[None] + colour_bias[:, None, None, None])
    emitted = (opacity * shading)[None] * colour
    return jnp.concatenate([emitted, optical[None]], 0)

def reference(density, light_vector, colour_gain, colour_bias, shear_step, reverse_view):
    extinction = EXTINCTION / NZ
    padded = jnp.pad(density, 1)

    def view_image(view):
        step = shear_step[view]
        backward = reverse_view[view]

        def advance(carry, index):
            colour_sum, optical = carry
            plane = jnp.where(backward == 1, NZ - 1 - index, index).astype(jnp.int32)
            block = lax.dynamic_slice_in_dim(padded, plane, 3, 0)
            fields = shade_block(block, light_vector, colour_gain, colour_bias, extinction)[:, 0]
            fields = jnp.pad(fields, ((0, 0), (0, SHEAR_MAX), (0, 0)))
            offset = (plane * step // NZ).astype(jnp.int32)
            sample = lax.dynamic_slice_in_dim(fields, offset, NY, 1)
            colour_sum = colour_sum + sample[:3] * jnp.exp(-optical)[None]
            optical = optical + sample[3]
            return ((colour_sum, optical), None)
        start = (jnp.zeros((3, NY, NX), jnp.float32), jnp.zeros((NY, NX), jnp.float32))
        (colour_sum, optical), _ = lax.scan(advance, start, jnp.arange(NZ, dtype=jnp.int32))
        return jnp.concatenate([colour_sum, -jnp.expm1(-optical)[None]], 0)
    return jnp.stack([view_image(view) for view in range(VIEWS)], 1)
```

```python
import functools

import jax
import jax.numpy as jnp
from jax import lax
from jax.experimental import pallas as pl
from jax.experimental.pallas import tpu as pltpu
from jax.sharding import PartitionSpec as P

EXTINCTION = 2.5
LEAD = 8
MESH = pl.DeviceIdType.MESH


def spans(low, high, size):
    return [(at, min(size, high - at)) for at in range(low, high, size)]


def kernel(
    groups,
    towers,
    density,
    light,
    gain,
    bias,
    shear,
    reverse,
    out,
    volume,
    fields,
    outgoing,
    incoming,
    local_sem,
    halo_send,
    halo_recv,
    part_send,
    part_recv,
):
    planes, rows, cols = density.shape
    margin = rows // 2
    views = shear.shape[0]
    share = rows // groups
    total_planes = planes * groups
    extinction = EXTINCTION / total_planes
    d = lax.axis_index("depth")
    h = lax.axis_index("height")
    end = LEAD + rows
    tall = end + margin

    own = pltpu.make_async_copy(
        density, volume.at[pl.ds(1, planes), pl.ds(LEAD, rows)], local_sem
    )
    own.start()

    def near(step_d, step_h):
        ok = None
        for at, step, count in ((d, step_d, groups), (h, step_h, towers)):
            if step:
                test = (at + step >= 0) & (at + step < count)
                ok = test if ok is None else ok & test
        return ok, (d + step_d, h + step_h)

    barrier = pltpu.get_barrier_semaphore()
    beside = [(0, 1), (0, -1), (1, 1), (1, -1), (-1, 1), (-1, -1)]
    expected = jnp.int32(groups - 1)
    for hop in range(1, groups):
        pl.semaphore_signal(
            barrier, inc=1, device_id=(lax.rem(d + hop, groups), h), device_id_type=MESH
        )
    for step_d, step_h in beside:
        ok, target = near(step_d, step_h)
        expected = expected + jnp.where(ok, 1, 0)

        @pl.when(ok)
        def _(target=target):
            pl.semaphore_signal(barrier, inc=1, device_id=target, device_id_type=MESH)

    @pl.when(d == 0)
    def _():
        volume[0] = jnp.zeros(volume.shape[1:], jnp.float32)

    @pl.when(d == groups - 1)
    def _():
        volume[planes + 1] = jnp.zeros(volume.shape[1:], jnp.float32)

    @pl.when(h == 0)
    def _():
        volume[1 : planes + 1, :LEAD] = jnp.zeros((planes, LEAD, cols), jnp.float32)

    @pl.when(h == towers - 1)
    def _():
        volume[:, end:tall] = jnp.zeros((planes + 2, margin, cols), jnp.float32)

    pl.semaphore_wait(barrier, expected)

    whole = pl.ds(0, planes)
    inner = pl.ds(1, planes)
    first, last = pl.ds(0, 1), pl.ds(planes - 1, 1)
    low, high = pl.ds(0, 1), pl.ds(planes + 1, 1)
    routes = [
        ((0, -1), whole, (0, margin), inner, end),
        ((1, -1), last, (0, margin), low, end),
        ((-1, -1), first, (0, margin), high, end),
        ((1, 0), last, (0, rows), low, LEAD),
        ((-1, 0), first, (0, rows), high, LEAD),
        ((0, 1), whole, (rows - LEAD, LEAD), inner, 0),
    ]

    def halo(index, reach):
        step, from_planes, (row, count), to_planes, to_row = routes[index]
        return pltpu.make_async_remote_copy(
            src_ref=density.at[from_planes, pl.ds(row, count)],
            dst_ref=volume.at[to_planes, pl.ds(to_row, count)],
            send_sem=halo_send.at[index],
            recv_sem=halo_recv.at[index],
            device_id=reach,
            device_id_type=MESH,
        )

    for index, route in enumerate(routes):
        ok, target = near(*route[0])

        @pl.when(ok)
        def _(index=index, target=target):
            halo(index, target).start()

    own.wait()

    lz, ly, lx = light[0], light[1], light[2]
    half_gain = [0.5 * gain[c] for c in range(3)]
    half_bias = [0.5 * bias[c] for c in range(3)]

    def shade(plane, row, count, keep):
        at = LEAD + row
        centre = volume[plane, at : at + count]
        lane = lax.broadcasted_iota(jnp.int32, (count, cols), 1)
        following = jnp.where(lane == cols - 1, 0.0, pltpu.roll(centre, cols - 1, 1))
        previous = jnp.where(lane == 0, 0.0, pltpu.roll(centre, 1, 1))
        dx = following - previous
        dz = volume[plane + 1, at : at + count] - volume[plane - 1, at : at + count]
        dy = volume[plane, at + 1 : at + 1 + count] - volume[plane, at - 1 : at - 1 + count]
        facing = (lz * dz + ly * dy + lx * dx) * lax.rsqrt(4.0 + dz * dz + dy * dy + dx * dx)
        shading = 0.25 + 1.5 * jnp.maximum(facing, 0.0)
        optical = extinction * (
            jnp.maximum(centre, 0.0) + jnp.log1p(jnp.exp(-jnp.abs(centre)))
        )
        opacity = jnp.tanh(0.5 * optical) * (1.0 + jnp.exp(-optical))
        if keep is not None:
            opacity = opacity * keep
        lit = 0.5 * (opacity * shading)
        to = pl.ds(row, count)
        for c in range(3):
            fields[c, plane - 1, to] = lit + lit * jnp.tanh(half_gain[c] * centre + half_bias[c])
        fields[3, plane - 1, to] = opacity

    inside = jnp.where(h < towers - 1, 1.0, 0.0)

    def early(plane, _):
        for row, count in spans(LEAD, rows - LEAD, 16):
            shade(plane, row, count, None)
        return 0

    lax.fori_loop(2, planes, early, 0)

    for index, route in enumerate(routes):
        step_d, step_h = route[0]
        ok, source = near(-step_d, -step_h)

        @pl.when(ok)
        def _(index=index, source=source):
            halo(index, source).wait_recv()

    def late(plane, _):
        shade(plane, 0, LEAD, None)
        shade(plane, rows - LEAD, LEAD, None)
        for row, count in spans(rows, rows + margin, 16):
            shade(plane, row, count, inside)
        return 0

    lax.fori_loop(1, planes + 1, late, 0)
    for plane in (1, planes):
        for row, count in spans(LEAD, rows - LEAD, 16):
            shade(plane, row, count, None)

    first_plane = d * planes

    def partial(view, block):
        step = shear[view]
        backward = reverse[view]
        colour = [jnp.zeros((share, cols), jnp.float32) for _ in range(3)]
        clear = jnp.ones((share, cols), jnp.float32)
        covered = jnp.zeros((share, cols), jnp.float32)
        for i in range(planes):
            plane = i + backward * (planes - 1 - 2 * i)
            offset = lax.div((first_plane + plane) * step, jnp.int32(total_planes))
            at = pl.ds(offset + block * share, share)
            for c in range(3):
                colour[c] = colour[c] + clear * fields[c, plane, at]
            covered = covered + clear * fields[3, plane, at]
            clear = 1.0 - covered
        return colour + [covered]

    def send(view, hop):
        peer = lax.rem(d + hop, groups)
        return pltpu.make_async_remote_copy(
            src_ref=outgoing.at[peer, view],
            dst_ref=incoming.at[d, view],
            send_sem=part_send.at[view, hop],
            recv_sem=part_recv.at[view, d],
            device_id=(peer, h),
            device_id_type=MESH,
        )

    for view in range(views):

        def one_peer(hop, _):
            peer = lax.rem(d + hop, groups)
            image = partial(view, peer)
            for c in range(4):
                outgoing[peer, view, c] = image[c]
            send(view, hop).start()
            return 0

        lax.fori_loop(1, groups, one_peer, 0)

    for view in range(views):
        image = partial(view, d)
        for c in range(4):
            incoming[d, view, c] = image[c]

    for view in range(views):

        def arrived(hop, _):
            source = lax.rem(d + hop, groups)
            pltpu.make_async_remote_copy(
                src_ref=outgoing.at[source, view],
                dst_ref=incoming.at[source, view],
                send_sem=part_send.at[view, hop],
                recv_sem=part_recv.at[view, source],
                device_id=(source, h),
                device_id_type=MESH,
            ).wait_recv()
            return 0

        lax.fori_loop(1, groups, arrived, 0)
        swap = reverse[view] == 1
        total = [incoming[0, view, c] for c in range(4)]
        for g in range(1, groups):
            new = [incoming[g, view, c] for c in range(4)]
            front = [jnp.where(swap, b, a) for a, b in zip(total, new)]
            behind = [jnp.where(swap, a, b) for a, b in zip(total, new)]
            clear = 1.0 - front[3]
            total = [f + clear * b for f, b in zip(front, behind)]
        for c in range(4):
            out[c, view] = total[c]

    for index, route in enumerate(routes):
        ok, target = near(*route[0])

        @pl.when(ok)
        def _(index=index, target=target):
            halo(index, target).wait_send()

    for view in range(views):

        def sent(hop, _):
            send(view, hop).wait_send()
            return 0

        lax.fori_loop(1, groups, sent, 0)


def on_device(groups, towers, density, light, gain, bias, shear, reverse):
    planes, rows, cols = density.shape
    views = shear.shape[0]
    share = rows // groups
    tall = LEAD + rows + rows // 2
    scalars = pl.BlockSpec(memory_space=pltpu.SMEM)
    return pl.pallas_call(
        functools.partial(kernel, groups, towers),
        name="render",
        out_shape=jax.ShapeDtypeStruct((4, views, share, cols), jnp.float32),
        in_specs=[pl.BlockSpec(memory_space=pl.ANY)] + [scalars] * 5,
        out_specs=pl.BlockSpec(memory_space=pltpu.VMEM),
        scratch_shapes=[
            pltpu.VMEM((planes + 2, tall + LEAD, cols), jnp.float32),
            pltpu.VMEM((4, planes, rows + rows // 2, cols), jnp.float32),
            pltpu.VMEM((groups, views, 4, share, cols), jnp.float32),
            pltpu.VMEM((groups, views, 4, share, cols), jnp.float32),
            pltpu.SemaphoreType.DMA,
            pltpu.SemaphoreType.DMA((6,)),
            pltpu.SemaphoreType.DMA((6,)),
            pltpu.SemaphoreType.DMA((views, groups)),
            pltpu.SemaphoreType.DMA((views, groups)),
        ],
        compiler_params=pltpu.CompilerParams(collective_id=0, has_side_effects=True),
    )(density, light, gain, bias, shear, reverse)


def solution(mesh):
    groups, towers = mesh.shape["depth"], mesh.shape["height"]
    placed = (P("depth", "height", None), P(), P(), P(), P(), P())
    return jax.shard_map(
        functools.partial(on_device, groups, towers),
        mesh=mesh,
        in_specs=placed,
        out_specs=P(None, None, ("height", "depth"), None),
        check_vma=False,
    )
```

```python
import functools

import jax
import jax.numpy as jnp
from jax import lax
from jax.experimental import pallas as pl
from jax.experimental.pallas import tpu as pltpu
from jax.sharding import PartitionSpec as P

EXTINCTION = 2.5
LEAD = 8
MESH = pl.DeviceIdType.MESH


def spans(low, high, size):
    return [(at, min(size, high - at)) for at in range(low, high, size)]


def kernel(
    groups,
    towers,
    density,
    light,
    gain,
    bias,
    shear,
    reverse,
    out,
    volume,
    fields,
    outgoing,
    incoming,
    handed,
    local_sem,
    halo_send,
    halo_recv,
    hand_send,
    hand_recv,
    part_send,
    part_recv,
):
    planes, rows, cols = density.shape
    margin = rows // 2
    views = shear.shape[0]
    share = rows // groups
    total_planes = planes * groups
    extinction = EXTINCTION / total_planes
    d = lax.axis_index("depth")
    h = lax.axis_index("height")
    end = LEAD + rows
    tall = end + margin

    own = pltpu.make_async_copy(
        density, volume.at[pl.ds(1, planes), pl.ds(LEAD, rows)], local_sem
    )
    own.start()

    def near(step_d, step_h):
        ok = None
        for at, step, count in ((d, step_d, groups), (h, step_h, towers)):
            if step:
                test = (at + step >= 0) & (at + step < count)
                ok = test if ok is None else ok & test
        return ok, (d + step_d, h + step_h)

    barrier = pltpu.get_barrier_semaphore()
    beside = [(0, 1), (0, -1), (1, 1), (1, -1), (-1, 1), (-1, -1)]
    expected = jnp.int32(groups - 1)
    for hop in range(1, groups):
        pl.semaphore_signal(
            barrier, inc=1, device_id=(lax.rem(d + hop, groups), h), device_id_type=MESH
        )
    for step_d, step_h in beside:
        ok, target = near(step_d, step_h)
        expected = expected + jnp.where(ok, 1, 0)

        @pl.when(ok)
        def _(target=target):
            pl.semaphore_signal(barrier, inc=1, device_id=target, device_id_type=MESH)

    @pl.when(d == 0)
    def _():
        volume[0] = jnp.zeros(volume.shape[1:], jnp.float32)

    @pl.when(d == groups - 1)
    def _():
        volume[planes + 1] = jnp.zeros(volume.shape[1:], jnp.float32)

    @pl.when(h == 0)
    def _():
        volume[1 : planes + 1, :LEAD] = jnp.zeros((planes, LEAD, cols), jnp.float32)

    @pl.when(h == towers - 1)
    def _():
        volume[:, end:tall] = jnp.zeros((planes + 2, margin, cols), jnp.float32)

    own.wait()

    lz, ly, lx = light[0], light[1], light[2]
    half_gain = [0.5 * gain[c] for c in range(3)]
    half_bias = [0.5 * bias[c] for c in range(3)]

    def shade(plane, row, count, keep):
        at = LEAD + row
        centre = volume[plane, at : at + count]
        lane = lax.broadcasted_iota(jnp.int32, (count, cols), 1)
        following = jnp.where(lane == cols - 1, 0.0, pltpu.roll(centre, cols - 1, 1))
        previous = jnp.where(lane == 0, 0.0, pltpu.roll(centre, 1, 1))
        dx = following - previous
        dz = volume[plane + 1, at : at + count] - volume[plane - 1, at : at + count]
        dy = volume[plane, at + 1 : at + 1 + count] - volume[plane, at - 1 : at - 1 + count]
        facing = (lz * dz + ly * dy + lx * dx) * lax.rsqrt(4.0 + dz * dz + dy * dy + dx * dx)
        shading = 0.25 + 1.5 * jnp.maximum(facing, 0.0)
        optical = extinction * (
            jnp.maximum(centre, 0.0) + jnp.log1p(jnp.exp(-jnp.abs(centre)))
        )
        opacity = jnp.tanh(0.5 * optical) * (1.0 + jnp.exp(-optical))
        if keep is not None:
            opacity = opacity * keep
        lit = 0.5 * (opacity * shading)
        to = pl.ds(row, count)
        for c in range(3):
            fields[c, plane - 1, to] = lit + lit * jnp.tanh(half_gain[c] * centre + half_bias[c])
        fields[3, plane - 1, to] = opacity

    inside = jnp.where(h < towers - 1, 1.0, 0.0)

    def early(plane, _):
        for row, count in spans(LEAD, rows - LEAD, 16):
            shade(plane, row, count, None)
        return 0

    lax.fori_loop(2, planes, early, 0)

    pl.semaphore_wait(barrier, expected)

    whole = pl.ds(0, planes)
    inner = pl.ds(1, planes)
    first, last = pl.ds(0, 1), pl.ds(planes - 1, 1)
    low, high = pl.ds(0, 1), pl.ds(planes + 1, 1)
    routes = [
        ((0, -1), whole, (0, margin), inner, end),
        ((1, -1), last, (0, margin), low, end),
        ((-1, -1), first, (0, margin), high, end),
        ((1, 0), last, (0, rows), low, LEAD),
        ((-1, 0), first, (0, rows), high, LEAD),
        ((0, 1), whole, (rows - LEAD, LEAD), inner, 0),
    ]

    def halo(index, reach):
        step, from_planes, (row, count), to_planes, to_row = routes[index]
        return pltpu.make_async_remote_copy(
            src_ref=density.at[from_planes, pl.ds(row, count)],
            dst_ref=volume.at[to_planes, pl.ds(to_row, count)],
            send_sem=halo_send.at[index],
            recv_sem=halo_recv.at[index],
            device_id=reach,
            device_id_type=MESH,
        )

    for index, route in enumerate(routes):
        ok, target = near(*route[0])

        @pl.when(ok)
        def _(index=index, target=target):
            halo(index, target).start()

    for index, route in enumerate(routes):
        step_d, step_h = route[0]
        ok, source = near(-step_d, -step_h)

        @pl.when(ok)
        def _(index=index, source=source):
            halo(index, source).wait_recv()

    def late(plane, _):
        shade(plane, 0, LEAD, None)
        shade(plane, rows - LEAD, LEAD, None)
        for row, count in spans(rows, rows + margin, 16):
            shade(plane, row, count, inside)
        return 0

    lax.fori_loop(1, planes + 1, late, 0)
    for plane in (1, planes):
        for row, count in spans(LEAD, rows - LEAD, 16):
            shade(plane, row, count, None)

    first_plane = d * planes

    def partial(view, block):
        step = shear[view]
        backward = reverse[view]
        colour = [jnp.zeros((share, cols), jnp.float32) for _ in range(3)]
        clear = jnp.ones((share, cols), jnp.float32)
        covered = jnp.zeros((share, cols), jnp.float32)
        for i in range(planes):
            plane = i + backward * (planes - 1 - 2 * i)
            offset = lax.div((first_plane + plane) * step, jnp.int32(total_planes))
            at = pl.ds(offset + block * share, share)
            for c in range(3):
                colour[c] = colour[c] + clear * fields[c, plane, at]
            covered = covered + clear * fields[3, plane, at]
            clear = 1.0 - covered
        return colour + [covered]

    odd = lax.rem(d, 2)
    out_step = 2 * odd - 1
    mate = d - out_step
    pair = lax.div(d, 2)
    beyond = odd * (groups - 1 - d) + (1 - odd) * d
    handing = odd * (d - 1) + (1 - odd) * (groups - 2 - d)

    def over(first, second, swap):
        front = [jnp.where(swap, b, a) for a, b in zip(first, second)]
        behind = [jnp.where(swap, a, b) for a, b in zip(first, second)]
        clear = 1.0 - front[3]
        return [f + clear * b for f, b in zip(front, behind)]

    def load(ref, block, view):
        return [ref[block, view, c] for c in range(4)]

    def store(ref, block, view, image):
        for c in range(4):
            ref[block, view, c] = image[c]

    def hand(view, block):
        return pltpu.make_async_remote_copy(
            src_ref=outgoing.at[block, view],
            dst_ref=handed.at[block, view],
            send_sem=hand_send.at[view, block],
            recv_sem=hand_recv.at[view, block],
            device_id=(mate, h),
            device_id_type=MESH,
        )

    def send(view, block):
        return pltpu.make_async_remote_copy(
            src_ref=outgoing.at[block, view],
            dst_ref=incoming.at[d, view],
            send_sem=part_send.at[view, block],
            recv_sem=part_recv.at[view, d],
            device_id=(block, h),
            device_id_type=MESH,
        )

    def receive(view, source):
        return pltpu.make_async_remote_copy(
            src_ref=outgoing.at[source, view],
            dst_ref=incoming.at[source, view],
            send_sem=part_send.at[view, source],
            recv_sem=part_recv.at[view, source],
            device_id=(source, h),
            device_id_type=MESH,
        )

    def each(count, body):
        def step(k, _):
            body(k)
            return 0

        lax.fori_loop(0, count, step, 0)

    def hand_over(view, k):
        block = d - out_step * (2 + k)
        store(outgoing, block, view, partial(view, block))
        hand(view, block).start()

    def prepare(view, k):
        block = d + out_step * (1 + k)
        store(outgoing, block, view, partial(view, block))

    def to_mate(view):
        store(outgoing, mate, view, partial(view, mate))
        send(view, mate).start()

    def pass_on(view, k):
        block = d + out_step * (1 + k)
        hand(view, block).wait_recv()
        own_part, other = load(outgoing, block, view), load(handed, block, view)
        swap = reverse[view] != odd
        store(outgoing, block, view, over(own_part, other, swap))
        send(view, block).start()

    each(views, lambda view: each(handing, lambda k: hand_over(view, k)))
    each(views, to_mate)
    each(views, lambda view: each(beyond, lambda k: prepare(view, k)))
    each(views, lambda view: store(incoming, d, view, partial(view, d)))
    each(views, lambda view: each(beyond, lambda k: pass_on(view, k)))

    def finish(view):
        swap = reverse[view] == 1
        receive(view, mate).wait_recv()
        both = over(load(incoming, d, view), load(incoming, mate, view), reverse[view] != odd)
        store(incoming, 2 * pair + 1, view, both)
        sources = [jnp.where(j > pair, 2 * j, 2 * j + 1) for j in range(groups // 2)]
        for j, source in enumerate(sources):

            @pl.when(j != pair)
            def _():
                receive(view, source).wait_recv()

        total = load(incoming, sources[0], view)
        for source in sources[1:]:
            total = over(total, load(incoming, source, view), swap)
        for c in range(4):
            out[c, view] = total[c]

    for view in range(views):
        finish(view)

    for index, route in enumerate(routes):
        ok, target = near(*route[0])

        @pl.when(ok)
        def _(index=index, target=target):
            halo(index, target).wait_send()

    def sent(view):
        send(view, mate).wait_send()
        each(handing, lambda k: hand(view, d - out_step * (2 + k)).wait_send())
        each(beyond, lambda k: send(view, d + out_step * (1 + k)).wait_send())

    each(views, sent)


def on_device(groups, towers, density, light, gain, bias, shear, reverse):
    planes, rows, cols = density.shape
    views = shear.shape[0]
    share = rows // groups
    tall = LEAD + rows + rows // 2
    scalars = pl.BlockSpec(memory_space=pltpu.SMEM)
    return pl.pallas_call(
        functools.partial(kernel, groups, towers),
        name="render",
        out_shape=jax.ShapeDtypeStruct((4, views, share, cols), jnp.float32),
        in_specs=[pl.BlockSpec(memory_space=pl.ANY)] + [scalars] * 5,
        out_specs=pl.BlockSpec(memory_space=pltpu.VMEM),
        scratch_shapes=[
            pltpu.VMEM((planes + 2, tall + LEAD, cols), jnp.float32),
            pltpu.VMEM((4, planes, rows + rows // 2, cols), jnp.float32),
            pltpu.VMEM((groups, views, 4, share, cols), jnp.float32),
            pltpu.VMEM((groups, views, 4, share, cols), jnp.float32),
            pltpu.VMEM((groups, views, 4, share, cols), jnp.float32),
            pltpu.SemaphoreType.DMA,
            pltpu.SemaphoreType.DMA((6,)),
            pltpu.SemaphoreType.DMA((6,)),
            pltpu.SemaphoreType.DMA((views, groups)),
            pltpu.SemaphoreType.DMA((views, groups)),
            pltpu.SemaphoreType.DMA((views, groups)),
            pltpu.SemaphoreType.DMA((views, groups)),
        ],
        compiler_params=pltpu.CompilerParams(collective_id=0, has_side_effects=True),
    )(density, light, gain, bias, shear, reverse)


def solution(mesh):
    groups, towers = mesh.shape["depth"], mesh.shape["height"]
    placed = (P("depth", "height", None), P(), P(), P(), P(), P())
    return jax.shard_map(
        functools.partial(on_device, groups, towers),
        mesh=mesh,
        in_specs=placed,
        out_specs=P(None, None, ("height", "depth"), None),
        check_vma=False,
    )
```

```python
import functools

import jax
import jax.numpy as jnp
from jax import lax
from jax.experimental import pallas as pl
from jax.experimental.pallas import tpu as pltpu
from jax.sharding import PartitionSpec as P

EXTINCTION = 2.5
LEAD = 8
MESH = pl.DeviceIdType.MESH


def spans(low, high, size):
    return [(at, min(size, high - at)) for at in range(low, high, size)]


def kernel(
    groups,
    towers,
    density,
    light,
    gain,
    bias,
    shear,
    reverse,
    out,
    volume,
    fields,
    outgoing,
    incoming,
    handed,
    local_sem,
    halo_send,
    halo_recv,
    hand_send,
    hand_recv,
    part_send,
    part_recv,
):
    planes, rows, cols = density.shape
    margin = rows // 2
    views = shear.shape[0]
    share = rows // groups
    total_planes = planes * groups
    extinction = EXTINCTION / total_planes
    d = lax.axis_index("depth")
    h = lax.axis_index("height")
    end = LEAD + rows
    tall = end + margin

    own = pltpu.make_async_copy(
        density, volume.at[pl.ds(1, planes), pl.ds(LEAD, rows)], local_sem
    )
    own.start()

    def near(step_d, step_h):
        ok = None
        for at, step, count in ((d, step_d, groups), (h, step_h, towers)):
            if step:
                test = (at + step >= 0) & (at + step < count)
                ok = test if ok is None else ok & test
        return ok, (d + step_d, h + step_h)

    barrier = pltpu.get_barrier_semaphore()
    beside = [(0, 1), (0, -1), (1, 1), (1, -1), (-1, 1), (-1, -1), (1, 0), (-1, 0)]
    if groups > 4:
        beside += [(step * hop, 0) for hop in range(2, groups) for step in (1, -1)]
    expected = jnp.int32(0)
    for step_d, step_h in beside:
        ok, target = near(step_d, step_h)
        expected = expected + jnp.where(ok, 1, 0)

        @pl.when(ok)
        def _(target=target):
            pl.semaphore_signal(barrier, inc=1, device_id=target, device_id_type=MESH)

    @pl.when(d == 0)
    def _():
        volume[0] = jnp.zeros(volume.shape[1:], jnp.float32)

    @pl.when(d == groups - 1)
    def _():
        volume[planes + 1] = jnp.zeros(volume.shape[1:], jnp.float32)

    @pl.when(h == 0)
    def _():
        volume[1 : planes + 1, :LEAD] = jnp.zeros((planes, LEAD, cols), jnp.float32)

    @pl.when(h == towers - 1)
    def _():
        volume[:, end:tall] = jnp.zeros((planes + 2, margin, cols), jnp.float32)

    own.wait()

    lz, ly, lx = light[0], light[1], light[2]
    half_gain = [0.5 * gain[c] for c in range(3)]
    half_bias = [0.5 * bias[c] for c in range(3)]

    def shade(plane, row, count, keep):
        at = LEAD + row
        centre = volume[plane, at : at + count]
        lane = lax.broadcasted_iota(jnp.int32, (count, cols), 1)
        following = jnp.where(lane == cols - 1, 0.0, pltpu.roll(centre, cols - 1, 1))
        previous = jnp.where(lane == 0, 0.0, pltpu.roll(centre, 1, 1))
        dx = following - previous
        dz = volume[plane + 1, at : at + count] - volume[plane - 1, at : at + count]
        dy = volume[plane, at + 1 : at + 1 + count] - volume[plane, at - 1 : at - 1 + count]
        facing = (lz * dz + ly * dy + lx * dx) * lax.rsqrt(4.0 + dz * dz + dy * dy + dx * dx)
        shading = 0.25 + 1.5 * jnp.maximum(facing, 0.0)
        optical = extinction * (
            jnp.maximum(centre, 0.0) + jnp.log1p(jnp.exp(-jnp.abs(centre)))
        )
        opacity = jnp.tanh(0.5 * optical) * (1.0 + jnp.exp(-optical))
        if keep is not None:
            opacity = opacity * keep
        lit = 0.5 * (opacity * shading)
        to = pl.ds(row, count)
        for c in range(3):
            fields[c, plane - 1, to] = lit + lit * jnp.tanh(half_gain[c] * centre + half_bias[c])
        fields[3, plane - 1, to] = opacity

    inside = jnp.where(h < towers - 1, 1.0, 0.0)

    def early(plane, _):
        for row, count in spans(LEAD, rows - LEAD, 16):
            shade(plane, row, count, None)
        return 0

    lax.fori_loop(2, planes, early, 0)

    pl.semaphore_wait(barrier, expected)

    whole = pl.ds(0, planes)
    inner = pl.ds(1, planes)
    first, last = pl.ds(0, 1), pl.ds(planes - 1, 1)
    low, high = pl.ds(0, 1), pl.ds(planes + 1, 1)
    routes = [
        ((0, -1), whole, (0, margin), inner, end),
        ((1, -1), last, (0, margin), low, end),
        ((-1, -1), first, (0, margin), high, end),
        ((1, 0), last, (0, rows), low, LEAD),
        ((-1, 0), first, (0, rows), high, LEAD),
        ((0, 1), whole, (rows - LEAD, LEAD), inner, 0),
    ]

    def halo(index, reach):
        step, from_planes, (row, count), to_planes, to_row = routes[index]
        return pltpu.make_async_remote_copy(
            src_ref=density.at[from_planes, pl.ds(row, count)],
            dst_ref=volume.at[to_planes, pl.ds(to_row, count)],
            send_sem=halo_send.at[index],
            recv_sem=halo_recv.at[index],
            device_id=reach,
            device_id_type=MESH,
        )

    for index, route in enumerate(routes):
        ok, target = near(*route[0])

        @pl.when(ok)
        def _(index=index, target=target):
            halo(index, target).start()

    for index, route in enumerate(routes):
        step_d, step_h = route[0]
        ok, source = near(-step_d, -step_h)

        @pl.when(ok)
        def _(index=index, source=source):
            halo(index, source).wait_recv()

    def late(plane, _):
        shade(plane, 0, LEAD, None)
        shade(plane, rows - LEAD, LEAD, None)
        for row, count in spans(rows, rows + margin, 16):
            shade(plane, row, count, inside)
        return 0

    lax.fori_loop(1, planes + 1, late, 0)
    for plane in (1, planes):
        for row, count in spans(LEAD, rows - LEAD, 16):
            shade(plane, row, count, None)

    first_plane = d * planes

    def partial(view, block):
        step = shear[view]
        backward = reverse[view]
        colour = [jnp.zeros((share, cols), jnp.float32) for _ in range(3)]
        clear = jnp.ones((share, cols), jnp.float32)
        covered = jnp.zeros((share, cols), jnp.float32)
        for i in range(planes):
            plane = i + backward * (planes - 1 - 2 * i)
            offset = lax.div((first_plane + plane) * step, jnp.int32(total_planes))
            at = pl.ds(offset + block * share, share)
            for c in range(3):
                colour[c] = colour[c] + clear * fields[c, plane, at]
            covered = covered + clear * fields[3, plane, at]
            clear = 1.0 - covered
        return colour + [covered]

    odd = lax.rem(d, 2)
    out_step = 2 * odd - 1
    mate = d - out_step
    pair = lax.div(d, 2)
    beyond = odd * (groups - 1 - d) + (1 - odd) * d
    handing = odd * (d - 1) + (1 - odd) * (groups - 2 - d)

    def over(first, second, swap):
        front = [jnp.where(swap, b, a) for a, b in zip(first, second)]
        behind = [jnp.where(swap, a, b) for a, b in zip(first, second)]
        clear = 1.0 - front[3]
        return [f + clear * b for f, b in zip(front, behind)]

    def load(ref, block, view):
        return [ref[block, view, c] for c in range(4)]

    def store(ref, block, view, image):
        for c in range(4):
            ref[block, view, c] = image[c]

    def hand(view, block):
        return pltpu.make_async_remote_copy(
            src_ref=outgoing.at[block, view],
            dst_ref=handed.at[block, view],
            send_sem=hand_send.at[view, block],
            recv_sem=hand_recv.at[view, block],
            device_id=(mate, h),
            device_id_type=MESH,
        )

    def send(view, block):
        return pltpu.make_async_remote_copy(
            src_ref=outgoing.at[block, view],
            dst_ref=incoming.at[d, view],
            send_sem=part_send.at[view, block],
            recv_sem=part_recv.at[view, d],
            device_id=(block, h),
            device_id_type=MESH,
        )

    def receive(view, source):
        return pltpu.make_async_remote_copy(
            src_ref=outgoing.at[source, view],
            dst_ref=incoming.at[source, view],
            send_sem=part_send.at[view, source],
            recv_sem=part_recv.at[view, source],
            device_id=(source, h),
            device_id_type=MESH,
        )

    def each(count, body):
        def step(k, _):
            body(k)
            return 0

        lax.fori_loop(0, count, step, 0)

    def hand_over(view, k):
        block = d - out_step * (2 + k)
        store(outgoing, block, view, partial(view, block))
        hand(view, block).start()

    def prepare(view, k):
        block = d + out_step * (1 + k)
        store(outgoing, block, view, partial(view, block))

    def to_mate(view):
        store(outgoing, mate, view, partial(view, mate))
        send(view, mate).start()

    def pass_on(view, k):
        block = d + out_step * (1 + k)
        hand(view, block).wait_recv()
        own_part, other = load(outgoing, block, view), load(handed, block, view)
        swap = reverse[view] != odd
        store(outgoing, block, view, over(own_part, other, swap))
        send(view, block).start()

    each(views, lambda view: each(handing, lambda k: hand_over(view, k)))
    each(views, to_mate)
    each(views, lambda view: each(beyond, lambda k: prepare(view, k)))
    each(views, lambda view: store(incoming, d, view, partial(view, d)))
    each(views, lambda view: each(beyond, lambda k: pass_on(view, k)))

    def finish(view):
        swap = reverse[view] == 1
        receive(view, mate).wait_recv()
        both = over(load(incoming, d, view), load(incoming, mate, view), reverse[view] != odd)
        store(incoming, 2 * pair + 1, view, both)
        sources = [jnp.where(j > pair, 2 * j, 2 * j + 1) for j in range(groups // 2)]
        for j, source in enumerate(sources):

            @pl.when(j != pair)
            def _():
                receive(view, source).wait_recv()

        total = load(incoming, sources[0], view)
        for source in sources[1:]:
            total = over(total, load(incoming, source, view), swap)
        for c in range(4):
            out[c, view] = total[c]

    for view in range(views):
        finish(view)

    for index, route in enumerate(routes):
        ok, target = near(*route[0])

        @pl.when(ok)
        def _(index=index, target=target):
            halo(index, target).wait_send()

    def sent(view):
        send(view, mate).wait_send()
        each(handing, lambda k: hand(view, d - out_step * (2 + k)).wait_send())
        each(beyond, lambda k: send(view, d + out_step * (1 + k)).wait_send())

    each(views, sent)


def on_device(groups, towers, density, light, gain, bias, shear, reverse):
    planes, rows, cols = density.shape
    views = shear.shape[0]
    share = rows // groups
    tall = LEAD + rows + rows // 2
    scalars = pl.BlockSpec(memory_space=pltpu.SMEM)
    return pl.pallas_call(
        functools.partial(kernel, groups, towers),
        name="render",
        out_shape=pltpu.VMEM((4, views, share, cols), jnp.float32),
        in_specs=[pl.BlockSpec(memory_space=pltpu.HBM)] + [scalars] * 5,
        out_specs=pl.BlockSpec(memory_space=pltpu.VMEM),
        scratch_shapes=[
            pltpu.VMEM((planes + 2, tall + LEAD, cols), jnp.float32),
            pltpu.VMEM((4, planes, rows + rows // 2, cols), jnp.float32),
            pltpu.VMEM((groups, views, 4, share, cols), jnp.float32),
            pltpu.VMEM((groups, views, 4, share, cols), jnp.float32),
            pltpu.VMEM((groups, views, 4, share, cols), jnp.float32),
            pltpu.SemaphoreType.DMA,
            pltpu.SemaphoreType.DMA((6,)),
            pltpu.SemaphoreType.DMA((6,)),
            pltpu.SemaphoreType.DMA((views, groups)),
            pltpu.SemaphoreType.DMA((views, groups)),
            pltpu.SemaphoreType.DMA((views, groups)),
            pltpu.SemaphoreType.DMA((views, groups)),
        ],
        compiler_params=pltpu.CompilerParams(collective_id=0, has_side_effects=True, vmem_limit_bytes=60 * 1024 * 1024),
    )(density, light, gain, bias, shear, reverse)


def solution(mesh):
    groups, towers = mesh.shape["depth"], mesh.shape["height"]
    placed = (P("depth", "height", None), P(), P(), P(), P(), P())
    return jax.shard_map(
        functools.partial(on_device, groups, towers),
        mesh=mesh,
        in_specs=placed,
        out_specs=P(None, None, ("height", "depth"), None),
        check_vma=False,
    )
```

```python
import functools

import jax
import jax.numpy as jnp
from jax import lax
from jax.experimental import pallas as pl
from jax.experimental.pallas import tpu as pltpu
from jax.sharding import PartitionSpec as P

EXTINCTION = 2.5
LEAD = 8
MESH = pl.DeviceIdType.MESH


def spans(low, high, size):
    return [(at, min(size, high - at)) for at in range(low, high, size)]


def kernel(
    groups,
    towers,
    density,
    light,
    gain,
    bias,
    shear,
    reverse,
    out,
    volume,
    fields,
    outgoing,
    incoming,
    handed,
    local_sem,
    halo_send,
    halo_recv,
    hand_send,
    hand_recv,
    part_send,
    part_recv,
):
    planes, rows, cols = density.shape
    margin = rows // 2
    views = shear.shape[0]
    share = rows // groups
    total_planes = planes * groups
    extinction = EXTINCTION / total_planes
    d = lax.axis_index("depth")
    h = lax.axis_index("height")
    end = LEAD + rows
    tall = end + margin

    own = pltpu.make_async_copy(
        density, volume.at[pl.ds(1, planes), pl.ds(LEAD, rows)], local_sem
    )
    own.start()

    def near(step_d, step_h):
        ok = None
        for at, step, count in ((d, step_d, groups), (h, step_h, towers)):
            if step:
                test = (at + step >= 0) & (at + step < count)
                ok = test if ok is None else ok & test
        return ok, (d + step_d, h + step_h)

    barrier = pltpu.get_barrier_semaphore()
    beside = [(0, 1), (0, -1), (1, 1), (1, -1), (-1, 1), (-1, -1), (1, 0), (-1, 0)]
    if groups > 4:
        beside += [(step * hop, 0) for hop in range(2, groups) for step in (1, -1)]
    expected = jnp.int32(0)
    for step_d, step_h in beside:
        ok, target = near(step_d, step_h)
        expected = expected + jnp.where(ok, 1, 0)

        @pl.when(ok)
        def _(target=target):
            pl.semaphore_signal(barrier, inc=1, device_id=target, device_id_type=MESH)

    pl.semaphore_wait(barrier, expected)

    whole = pl.ds(0, planes)
    inner = pl.ds(1, planes)
    first, last = pl.ds(0, 1), pl.ds(planes - 1, 1)
    low, high = pl.ds(0, 1), pl.ds(planes + 1, 1)
    routes = [
        ((0, -1), whole, (0, margin), inner, end),
        ((1, -1), last, (0, margin), low, end),
        ((-1, -1), first, (0, margin), high, end),
        ((1, 0), last, (0, rows), low, LEAD),
        ((-1, 0), first, (0, rows), high, LEAD),
        ((0, 1), whole, (rows - LEAD, LEAD), inner, 0),
    ]

    def halo(index, reach):
        step, from_planes, (row, count), to_planes, to_row = routes[index]
        return pltpu.make_async_remote_copy(
            src_ref=density.at[from_planes, pl.ds(row, count)],
            dst_ref=volume.at[to_planes, pl.ds(to_row, count)],
            send_sem=halo_send.at[index],
            recv_sem=halo_recv.at[index],
            device_id=reach,
            device_id_type=MESH,
        )

    for index, route in enumerate(routes):
        ok, target = near(*route[0])

        @pl.when(ok)
        def _(index=index, target=target):
            halo(index, target).start()

    @pl.when(d == 0)
    def _():
        volume[0] = jnp.zeros(volume.shape[1:], jnp.float32)

    @pl.when(d == groups - 1)
    def _():
        volume[planes + 1] = jnp.zeros(volume.shape[1:], jnp.float32)

    @pl.when(h == 0)
    def _():
        volume[1 : planes + 1, :LEAD] = jnp.zeros((planes, LEAD, cols), jnp.float32)

    @pl.when(h == towers - 1)
    def _():
        volume[:, end:tall] = jnp.zeros((planes + 2, margin, cols), jnp.float32)

    own.wait()

    lz, ly, lx = light[0], light[1], light[2]
    half_gain = [0.5 * gain[c] for c in range(3)]
    half_bias = [0.5 * bias[c] for c in range(3)]

    def shade(plane, row, count, keep):
        at = LEAD + row
        centre = volume[plane, at : at + count]
        lane = lax.broadcasted_iota(jnp.int32, (count, cols), 1)
        following = jnp.where(lane == cols - 1, 0.0, pltpu.roll(centre, cols - 1, 1))
        previous = jnp.where(lane == 0, 0.0, pltpu.roll(centre, 1, 1))
        dx = following - previous
        dz = volume[plane + 1, at : at + count] - volume[plane - 1, at : at + count]
        dy = volume[plane, at + 1 : at + 1 + count] - volume[plane, at - 1 : at - 1 + count]
        facing = (lz * dz + ly * dy + lx * dx) * lax.rsqrt(4.0 + dz * dz + dy * dy + dx * dx)
        shading = 0.25 + 1.5 * jnp.maximum(facing, 0.0)
        optical = extinction * (
            jnp.maximum(centre, 0.0) + jnp.log1p(jnp.exp(-jnp.abs(centre)))
        )
        opacity = jnp.tanh(0.5 * optical) * (1.0 + jnp.exp(-optical))
        if keep is not None:
            opacity = opacity * keep
        lit = 0.5 * (opacity * shading)
        to = pl.ds(row, count)
        for c in range(3):
            fields[c, plane - 1, to] = lit + lit * jnp.tanh(half_gain[c] * centre + half_bias[c])
        fields[3, plane - 1, to] = opacity

    inside = jnp.where(h < towers - 1, 1.0, 0.0)

    def early(plane, _):
        for row, count in spans(LEAD, rows - LEAD, 16):
            shade(plane, row, count, None)
        return 0

    lax.fori_loop(2, planes, early, 0)

    for index, route in enumerate(routes):
        step_d, step_h = route[0]
        ok, source = near(-step_d, -step_h)

        @pl.when(ok)
        def _(index=index, source=source):
            halo(index, source).wait_recv()

    def late(plane, _):
        shade(plane, 0, LEAD, None)
        shade(plane, rows - LEAD, LEAD, None)
        for row, count in spans(rows, rows + margin, 16):
            shade(plane, row, count, inside)
        return 0

    lax.fori_loop(1, planes + 1, late, 0)
    for plane in (1, planes):
        for row, count in spans(LEAD, rows - LEAD, 16):
            shade(plane, row, count, None)

    first_plane = d * planes

    def partial(view, block):
        step = shear[view]
        backward = reverse[view]
        colour = [jnp.zeros((share, cols), jnp.float32) for _ in range(3)]
        clear = jnp.ones((share, cols), jnp.float32)
        covered = jnp.zeros((share, cols), jnp.float32)
        for i in range(planes):
            plane = i + backward * (planes - 1 - 2 * i)
            offset = lax.div((first_plane + plane) * step, jnp.int32(total_planes))
            at = pl.ds(offset + block * share, share)
            for c in range(3):
                colour[c] = colour[c] + clear * fields[c, plane, at]
            covered = covered + clear * fields[3, plane, at]
            clear = 1.0 - covered
        return colour + [covered]

    odd = lax.rem(d, 2)
    out_step = 2 * odd - 1
    mate = d - out_step
    pair = lax.div(d, 2)
    beyond = odd * (groups - 1 - d) + (1 - odd) * d
    handing = odd * (d - 1) + (1 - odd) * (groups - 2 - d)

    def over(first, second, swap):
        front = [jnp.where(swap, b, a) for a, b in zip(first, second)]
        behind = [jnp.where(swap, a, b) for a, b in zip(first, second)]
        clear = 1.0 - front[3]
        return [f + clear * b for f, b in zip(front, behind)]

    def load(ref, block, view):
        return [ref[block, view, c] for c in range(4)]

    def store(ref, block, view, image):
        for c in range(4):
            ref[block, view, c] = image[c]

    def hand(view, block):
        return pltpu.make_async_remote_copy(
            src_ref=outgoing.at[block, view],
            dst_ref=handed.at[block, view],
            send_sem=hand_send.at[view, block],
            recv_sem=hand_recv.at[view, block],
            device_id=(mate, h),
            device_id_type=MESH,
        )

    def send(view, block):
        return pltpu.make_async_remote_copy(
            src_ref=outgoing.at[block, view],
            dst_ref=incoming.at[d, view],
            send_sem=part_send.at[view, block],
            recv_sem=part_recv.at[view, d],
            device_id=(block, h),
            device_id_type=MESH,
        )

    def receive(view, source):
        return pltpu.make_async_remote_copy(
            src_ref=outgoing.at[source, view],
            dst_ref=incoming.at[source, view],
            send_sem=part_send.at[view, source],
            recv_sem=part_recv.at[view, source],
            device_id=(source, h),
            device_id_type=MESH,
        )

    def each(count, body):
        def step(k, _):
            body(k)
            return 0

        lax.fori_loop(0, count, step, 0)

    def hand_over(view, k):
        block = odd * k + (1 - odd) * (groups - 1 - k)
        store(outgoing, block, view, partial(view, block))
        hand(view, block).start()

    def prepare(view, k):
        block = d + out_step * (1 + k)
        store(outgoing, block, view, partial(view, block))

    def to_mate(view):
        store(outgoing, mate, view, partial(view, mate))
        send(view, mate).start()

    def pass_on(view, k):
        block = odd * (groups - 1 - k) + (1 - odd) * k
        hand(view, block).wait_recv()
        own_part, other = load(outgoing, block, view), load(handed, block, view)
        swap = reverse[view] != odd
        store(outgoing, block, view, over(own_part, other, swap))
        send(view, block).start()

    each(handing, lambda k: each(views, lambda view: hand_over(view, k)))
    each(views, to_mate)
    each(views, lambda view: each(beyond, lambda k: prepare(view, k)))
    each(views, lambda view: store(incoming, d, view, partial(view, d)))
    each(beyond, lambda k: each(views, lambda view: pass_on(view, k)))

    def finish(view):
        swap = reverse[view] == 1
        receive(view, mate).wait_recv()
        both = over(load(incoming, d, view), load(incoming, mate, view), reverse[view] != odd)
        store(incoming, 2 * pair + 1, view, both)
        sources = [jnp.where(j > pair, 2 * j, 2 * j + 1) for j in range(groups // 2)]
        for j, source in enumerate(sources):

            @pl.when(j != pair)
            def _():
                receive(view, source).wait_recv()

        total = load(incoming, sources[0], view)
        for source in sources[1:]:
            total = over(total, load(incoming, source, view), swap)
        for c in range(4):
            out[c, view] = total[c]

    for view in range(views):
        finish(view)

    for index, route in enumerate(routes):
        ok, target = near(*route[0])

        @pl.when(ok)
        def _(index=index, target=target):
            halo(index, target).wait_send()

    def sent(view):
        send(view, mate).wait_send()
        each(handing, lambda k: hand(view, d - out_step * (2 + k)).wait_send())
        each(beyond, lambda k: send(view, d + out_step * (1 + k)).wait_send())

    each(views, sent)


def on_device(groups, towers, density, light, gain, bias, shear, reverse):
    planes, rows, cols = density.shape
    views = shear.shape[0]
    share = rows // groups
    tall = LEAD + rows + rows // 2
    scalars = pl.BlockSpec(memory_space=pltpu.SMEM)
    return pl.pallas_call(
        functools.partial(kernel, groups, towers),
        name="render",
        out_shape=pltpu.VMEM((4, views, share, cols), jnp.float32),
        in_specs=[pl.BlockSpec(memory_space=pltpu.HBM)] + [scalars] * 5,
        out_specs=pl.BlockSpec(memory_space=pltpu.VMEM),
        scratch_shapes=[
            pltpu.VMEM((planes + 2, tall + LEAD, cols), jnp.float32),
            pltpu.VMEM((4, planes, rows + rows // 2, cols), jnp.float32),
            pltpu.VMEM((groups, views, 4, share, cols), jnp.float32),
            pltpu.VMEM((groups, views, 4, share, cols), jnp.float32),
            pltpu.VMEM((groups, views, 4, share, cols), jnp.float32),
            pltpu.SemaphoreType.DMA,
            pltpu.SemaphoreType.DMA((6,)),
            pltpu.SemaphoreType.DMA((6,)),
            pltpu.SemaphoreType.DMA((views, groups)),
            pltpu.SemaphoreType.DMA((views, groups)),
            pltpu.SemaphoreType.DMA((views, groups)),
            pltpu.SemaphoreType.DMA((views, groups)),
        ],
        compiler_params=pltpu.CompilerParams(collective_id=0, has_side_effects=True, vmem_limit_bytes=60 * 1024 * 1024),
    )(density, light, gain, bias, shear, reverse)


def solution(mesh):
    groups, towers = mesh.shape["depth"], mesh.shape["height"]
    placed = (P("depth", "height", None), P(), P(), P(), P(), P())
    return jax.shard_map(
        functools.partial(on_device, groups, towers),
        mesh=mesh,
        in_specs=placed,
        out_specs=P(None, None, ("height", "depth"), None),
        check_vma=False,
    )
```

```python
import functools

import jax
import jax.numpy as jnp
from jax import lax
from jax.experimental import pallas as pl
from jax.experimental.pallas import tpu as pltpu
from jax.sharding import PartitionSpec as P

EXTINCTION = 2.5
LEAD = 8
MESH = pl.DeviceIdType.MESH


def spans(low, high, size):
    return [(at, min(size, high - at)) for at in range(low, high, size)]


def kernel(
    groups,
    towers,
    density,
    light,
    gain,
    bias,
    shear,
    reverse,
    out,
    volume,
    fields,
    outgoing,
    incoming,
    handed,
    local_sem,
    halo_send,
    halo_recv,
    hand_send,
    hand_recv,
    part_send,
    part_recv,
):
    planes, rows, cols = density.shape
    margin = rows // 2
    views = shear.shape[0]
    share = rows // groups
    total_planes = planes * groups
    extinction = EXTINCTION / total_planes
    d = lax.axis_index("depth")
    h = lax.axis_index("height")
    end = LEAD + rows
    tall = end + margin

    own = pltpu.make_async_copy(
        density, volume.at[pl.ds(1, planes), pl.ds(LEAD, rows)], local_sem
    )
    own.start()

    def near(step_d, step_h):
        ok = None
        for at, step, count in ((d, step_d, groups), (h, step_h, towers)):
            if step:
                test = (at + step >= 0) & (at + step < count)
                ok = test if ok is None else ok & test
        return ok, (d + step_d, h + step_h)

    barrier = pltpu.get_barrier_semaphore()
    beside = [(0, 1), (0, -1), (1, 1), (1, -1), (-1, 1), (-1, -1), (1, 0), (-1, 0)]
    if groups > 4:
        beside += [(step * hop, 0) for hop in range(2, groups) for step in (1, -1)]
    expected = jnp.int32(0)
    for step_d, step_h in beside:
        ok, target = near(step_d, step_h)
        expected = expected + jnp.where(ok, 1, 0)

        @pl.when(ok)
        def _(target=target):
            pl.semaphore_signal(barrier, inc=1, device_id=target, device_id_type=MESH)

    pl.semaphore_wait(barrier, expected)

    whole = pl.ds(0, planes)
    inner = pl.ds(1, planes)
    first, last = pl.ds(0, 1), pl.ds(planes - 1, 1)
    low, high = pl.ds(0, 1), pl.ds(planes + 1, 1)
    routes = [
        ((0, -1), whole, (0, margin), inner, end),
        ((1, -1), last, (0, margin), low, end),
        ((-1, -1), first, (0, margin), high, end),
        ((1, 0), last, (0, rows), low, LEAD),
        ((-1, 0), first, (0, rows), high, LEAD),
        ((0, 1), whole, (rows - LEAD, LEAD), inner, 0),
    ]

    def halo(index, reach):
        step, from_planes, (row, count), to_planes, to_row = routes[index]
        return pltpu.make_async_remote_copy(
            src_ref=density.at[from_planes, pl.ds(row, count)],
            dst_ref=volume.at[to_planes, pl.ds(to_row, count)],
            send_sem=halo_send.at[index],
            recv_sem=halo_recv.at[index],
            device_id=reach,
            device_id_type=MESH,
        )

    for index, route in enumerate(routes):
        ok, target = near(*route[0])

        @pl.when(ok)
        def _(index=index, target=target):
            halo(index, target).start()

    @pl.when(d == 0)
    def _():
        volume[0] = jnp.zeros(volume.shape[1:], jnp.float32)

    @pl.when(d == groups - 1)
    def _():
        volume[planes + 1] = jnp.zeros(volume.shape[1:], jnp.float32)

    @pl.when(h == 0)
    def _():
        volume[1 : planes + 1, :LEAD] = jnp.zeros((planes, LEAD, cols), jnp.float32)

    @pl.when(h == towers - 1)
    def _():
        volume[:, end:tall] = jnp.zeros((planes + 2, margin, cols), jnp.float32)

    own.wait()

    lz, ly, lx = light[0], light[1], light[2]
    half_gain = [0.5 * gain[c] for c in range(3)]
    half_bias = [0.5 * bias[c] for c in range(3)]

    def shade(plane, row, count, keep):
        at = LEAD + row
        centre = volume[plane, at : at + count]
        lane = lax.broadcasted_iota(jnp.int32, (count, cols), 1)
        following = jnp.where(lane == cols - 1, 0.0, pltpu.roll(centre, cols - 1, 1))
        previous = jnp.where(lane == 0, 0.0, pltpu.roll(centre, 1, 1))
        dx = following - previous
        dz = volume[plane + 1, at : at + count] - volume[plane - 1, at : at + count]
        dy = volume[plane, at + 1 : at + 1 + count] - volume[plane, at - 1 : at - 1 + count]
        facing = (lz * dz + ly * dy + lx * dx) * lax.rsqrt(4.0 + dz * dz + dy * dy + dx * dx)
        shading = 0.25 + 1.5 * jnp.maximum(facing, 0.0)
        optical = extinction * (
            jnp.maximum(centre, 0.0) + jnp.log1p(jnp.exp(-jnp.abs(centre)))
        )
        opacity = jnp.tanh(0.5 * optical) * (1.0 + jnp.exp(-optical))
        if keep is not None:
            opacity = opacity * keep
        lit = 0.5 * (opacity * shading)
        to = pl.ds(row, count)
        for c in range(3):
            fields[c, plane - 1, to] = lit + lit * jnp.tanh(half_gain[c] * centre + half_bias[c])
        fields[3, plane - 1, to] = opacity

    inside = jnp.where(h < towers - 1, 1.0, 0.0)

    def early(plane, _):
        for row, count in spans(LEAD, rows - LEAD, 16):
            shade(plane, row, count, None)
        return 0

    lax.fori_loop(2, planes, early, 0)

    def landed(index):
        step_d, step_h = routes[index][0]
        ok, source = near(-step_d, -step_h)

        @pl.when(ok)
        def _():
            halo(index, source).wait_recv()

    def shade_low():
        for index in (3, 4, 5):
            landed(index)
        for plane in range(1, planes + 1):
            shade(plane, 0, LEAD, None)
        for row, count in spans(LEAD, rows - LEAD, 16):
            for plane in (1, planes):
                shade(plane, row, count, None)

    def shade_high():
        for index in (0, 1, 2):
            landed(index)

        def bottom(at, _):
            for plane in (2 * at + 1, 2 * at + 2):
                shade(plane, rows - LEAD, LEAD, None)
                for row, count in spans(rows, rows + margin, 16):
                    shade(plane, row, count, inside)
            return 0

        lax.fori_loop(0, planes // 2, bottom, 0)

    first_plane = d * planes

    def partial(view, block):
        step = shear[view]
        backward = reverse[view]
        colour = [jnp.zeros((share, cols), jnp.float32) for _ in range(3)]
        clear = jnp.ones((share, cols), jnp.float32)
        covered = jnp.zeros((share, cols), jnp.float32)
        for i in range(planes):
            plane = i + backward * (planes - 1 - 2 * i)
            offset = lax.div((first_plane + plane) * step, jnp.int32(total_planes))
            at = pl.ds(offset + block * share, share)
            for c in range(3):
                colour[c] = colour[c] + clear * fields[c, plane, at]
            covered = covered + clear * fields[3, plane, at]
            clear = 1.0 - covered
        return colour + [covered]

    odd = lax.rem(d, 2)
    out_step = 2 * odd - 1
    mate = d - out_step
    pair = lax.div(d, 2)
    beyond = odd * (groups - 1 - d) + (1 - odd) * d
    handing = odd * (d - 1) + (1 - odd) * (groups - 2 - d)

    def over(first, second, swap):
        front = [jnp.where(swap, b, a) for a, b in zip(first, second)]
        behind = [jnp.where(swap, a, b) for a, b in zip(first, second)]
        clear = 1.0 - front[3]
        return [f + clear * b for f, b in zip(front, behind)]

    def load(ref, block, view):
        return [ref[block, view, c] for c in range(4)]

    def store(ref, block, view, image):
        for c in range(4):
            ref[block, view, c] = image[c]

    def hand(view, block):
        return pltpu.make_async_remote_copy(
            src_ref=outgoing.at[block, view],
            dst_ref=handed.at[block, view],
            send_sem=hand_send.at[view, block],
            recv_sem=hand_recv.at[view, block],
            device_id=(mate, h),
            device_id_type=MESH,
        )

    def send(view, block):
        return pltpu.make_async_remote_copy(
            src_ref=outgoing.at[block, view],
            dst_ref=incoming.at[d, view],
            send_sem=part_send.at[view, block],
            recv_sem=part_recv.at[view, d],
            device_id=(block, h),
            device_id_type=MESH,
        )

    def receive(view, source):
        return pltpu.make_async_remote_copy(
            src_ref=outgoing.at[source, view],
            dst_ref=incoming.at[source, view],
            send_sem=part_send.at[view, source],
            recv_sem=part_recv.at[view, source],
            device_id=(source, h),
            device_id_type=MESH,
        )

    def each(count, body):
        def step(k, _):
            body(k)
            return 0

        lax.fori_loop(0, count, step, 0)

    def hand_over(view, k):
        block = odd * k + (1 - odd) * (groups - 1 - k)
        store(outgoing, block, view, partial(view, block))
        hand(view, block).start()

    def prepare(view, k):
        block = d + out_step * (1 + k)
        store(outgoing, block, view, partial(view, block))

    def to_mate(view):
        store(outgoing, mate, view, partial(view, mate))
        send(view, mate).start()

    def pass_on(view, k):
        block = odd * (groups - 1 - k) + (1 - odd) * k
        hand(view, block).wait_recv()
        own_part, other = load(outgoing, block, view), load(handed, block, view)
        swap = reverse[view] != odd
        store(outgoing, block, view, over(own_part, other, swap))
        send(view, block).start()

    reach = lax.div((first_plane + planes - 1) * margin, jnp.int32(total_planes))

    def hand_round(early):
        def one(k):
            block = odd * k + (1 - odd) * (groups - 1 - k)
            ready = ((block + 1) * share + reach <= rows - LEAD) & (odd == 1)

            @pl.when(ready if early else jnp.logical_not(ready))
            def _():
                each(views, lambda view: hand_over(view, k))

        each(handing, one)

    shade_low()
    hand_round(True)
    shade_high()
    hand_round(False)
    each(views, to_mate)
    each(views, lambda view: each(beyond, lambda k: prepare(view, k)))
    each(views, lambda view: store(incoming, d, view, partial(view, d)))
    each(beyond, lambda k: each(views, lambda view: pass_on(view, k)))

    def finish(view):
        swap = reverse[view] == 1
        receive(view, mate).wait_recv()
        both = over(load(incoming, d, view), load(incoming, mate, view), reverse[view] != odd)
        store(incoming, 2 * pair + 1, view, both)
        sources = [jnp.where(j > pair, 2 * j, 2 * j + 1) for j in range(groups // 2)]
        for j, source in enumerate(sources):

            @pl.when(j != pair)
            def _():
                receive(view, source).wait_recv()

        total = load(incoming, sources[0], view)
        for source in sources[1:]:
            total = over(total, load(incoming, source, view), swap)
        for c in range(4):
            out[c, view] = total[c]

    for view in range(views):
        finish(view)

    for index, route in enumerate(routes):
        ok, target = near(*route[0])

        @pl.when(ok)
        def _(index=index, target=target):
            halo(index, target).wait_send()

    def sent(view):
        send(view, mate).wait_send()
        each(handing, lambda k: hand(view, d - out_step * (2 + k)).wait_send())
        each(beyond, lambda k: send(view, d + out_step * (1 + k)).wait_send())

    each(views, sent)


def on_device(groups, towers, density, light, gain, bias, shear, reverse):
    planes, rows, cols = density.shape
    views = shear.shape[0]
    share = rows // groups
    tall = LEAD + rows + rows // 2
    scalars = pl.BlockSpec(memory_space=pltpu.SMEM)
    return pl.pallas_call(
        functools.partial(kernel, groups, towers),
        name="render",
        out_shape=pltpu.VMEM((4, views, share, cols), jnp.float32),
        in_specs=[pl.BlockSpec(memory_space=pltpu.HBM)] + [scalars] * 5,
        out_specs=pl.BlockSpec(memory_space=pltpu.VMEM),
        scratch_shapes=[
            pltpu.VMEM((planes + 2, tall + LEAD, cols), jnp.float32),
            pltpu.VMEM((4, planes, rows + rows // 2, cols), jnp.float32),
            pltpu.VMEM((groups, views, 4, share, cols), jnp.float32),
            pltpu.VMEM((groups, views, 4, share, cols), jnp.float32),
            pltpu.VMEM((groups, views, 4, share, cols), jnp.float32),
            pltpu.SemaphoreType.DMA,
            pltpu.SemaphoreType.DMA((6,)),
            pltpu.SemaphoreType.DMA((6,)),
            pltpu.SemaphoreType.DMA((views, groups)),
            pltpu.SemaphoreType.DMA((views, groups)),
            pltpu.SemaphoreType.DMA((views, groups)),
            pltpu.SemaphoreType.DMA((views, groups)),
        ],
        compiler_params=pltpu.CompilerParams(collective_id=0, has_side_effects=True, vmem_limit_bytes=60 * 1024 * 1024),
    )(density, light, gain, bias, shear, reverse)


def solution(mesh):
    groups, towers = mesh.shape["depth"], mesh.shape["height"]
    placed = (P("depth", "height", None), P(), P(), P(), P(), P())
    return jax.shard_map(
        functools.partial(on_device, groups, towers),
        mesh=mesh,
        in_specs=placed,
        out_specs=P(None, None, ("height", "depth"), None),
        check_vma=False,
    )
```

```python
import functools

import jax
import jax.numpy as jnp
from jax import lax
from jax.experimental import pallas as pl
from jax.experimental.pallas import tpu as pltpu
from jax.sharding import PartitionSpec as P

EXTINCTION = 2.5
LEAD = 8
MESH = pl.DeviceIdType.MESH


def spans(low, high, size):
    return [(at, min(size, high - at)) for at in range(low, high, size)]


def kernel(
    groups,
    towers,
    density,
    light,
    gain,
    bias,
    shear,
    reverse,
    out,
    volume,
    fields,
    outgoing,
    incoming,
    handed,
    local_sem,
    halo_send,
    halo_recv,
    hand_send,
    hand_recv,
    part_send,
    part_recv,
):
    planes, rows, cols = density.shape
    margin = rows // 2
    views = shear.shape[0]
    share = rows // groups
    total_planes = planes * groups
    extinction = EXTINCTION / total_planes
    d = lax.axis_index("depth")
    h = lax.axis_index("height")
    end = LEAD + rows
    tall = end + margin

    own = pltpu.make_async_copy(
        density, volume.at[pl.ds(1, planes), pl.ds(LEAD, rows)], local_sem
    )
    own.start()

    def near(step_d, step_h):
        ok = None
        for at, step, count in ((d, step_d, groups), (h, step_h, towers)):
            if step:
                test = (at + step >= 0) & (at + step < count)
                ok = test if ok is None else ok & test
        return ok, (d + step_d, h + step_h)

    barrier = pltpu.get_barrier_semaphore()
    beside = [(0, 1), (0, -1), (1, 1), (1, -1), (-1, 1), (-1, -1), (1, 0), (-1, 0)]
    if groups > 4:
        beside += [(step * hop, 0) for hop in range(2, groups) for step in (1, -1)]
    expected = jnp.int32(0)
    for step_d, step_h in beside:
        ok, target = near(step_d, step_h)
        expected = expected + jnp.where(ok, 1, 0)

        @pl.when(ok)
        def _(target=target):
            pl.semaphore_signal(barrier, inc=1, device_id=target, device_id_type=MESH)

    pl.semaphore_wait(barrier, expected)

    whole = pl.ds(0, planes)
    inner = pl.ds(1, planes)
    first, last = pl.ds(0, 1), pl.ds(planes - 1, 1)
    low, high = pl.ds(0, 1), pl.ds(planes + 1, 1)
    routes = [
        ((1, 0), last, (0, rows), low, LEAD),
        ((-1, 0), first, (0, rows), high, LEAD),
        ((0, 1), whole, (rows - LEAD, LEAD), inner, 0),
        ((0, -1), whole, (0, margin), inner, end),
        ((1, -1), last, (0, margin), low, end),
        ((-1, -1), first, (0, margin), high, end),
    ]

    def halo(index, reach):
        step, from_planes, (row, count), to_planes, to_row = routes[index]
        return pltpu.make_async_remote_copy(
            src_ref=density.at[from_planes, pl.ds(row, count)],
            dst_ref=volume.at[to_planes, pl.ds(to_row, count)],
            send_sem=halo_send.at[index],
            recv_sem=halo_recv.at[index],
            device_id=reach,
            device_id_type=MESH,
        )

    for index, route in enumerate(routes):
        ok, target = near(*route[0])

        @pl.when(ok)
        def _(index=index, target=target):
            halo(index, target).start()

    @pl.when(d == 0)
    def _():
        volume[0] = jnp.zeros(volume.shape[1:], jnp.float32)

    @pl.when(d == groups - 1)
    def _():
        volume[planes + 1] = jnp.zeros(volume.shape[1:], jnp.float32)

    @pl.when(h == 0)
    def _():
        volume[1 : planes + 1, :LEAD] = jnp.zeros((planes, LEAD, cols), jnp.float32)

    @pl.when(h == towers - 1)
    def _():
        volume[:, end:tall] = jnp.zeros((planes + 2, margin, cols), jnp.float32)

    own.wait()

    lz, ly, lx = light[0], light[1], light[2]
    half_gain = [0.5 * gain[c] for c in range(3)]
    half_bias = [0.5 * bias[c] for c in range(3)]

    def shade(plane, row, count, keep):
        at = LEAD + row
        centre = volume[plane, at : at + count]
        lane = lax.broadcasted_iota(jnp.int32, (count, cols), 1)
        following = jnp.where(lane == cols - 1, 0.0, pltpu.roll(centre, cols - 1, 1))
        previous = jnp.where(lane == 0, 0.0, pltpu.roll(centre, 1, 1))
        dx = following - previous
        dz = volume[plane + 1, at : at + count] - volume[plane - 1, at : at + count]
        dy = volume[plane, at + 1 : at + 1 + count] - volume[plane, at - 1 : at - 1 + count]
        facing = (lz * dz + ly * dy + lx * dx) * lax.rsqrt(4.0 + dz * dz + dy * dy + dx * dx)
        shading = 0.25 + 1.5 * jnp.maximum(facing, 0.0)
        optical = extinction * (
            jnp.maximum(centre, 0.0) + jnp.log1p(jnp.exp(-jnp.abs(centre)))
        )
        opacity = jnp.tanh(0.5 * optical) * (1.0 + jnp.exp(-optical))
        if keep is not None:
            opacity = opacity * keep
        lit = 0.5 * (opacity * shading)
        to = pl.ds(row, count)
        for c in range(3):
            fields[c, plane - 1, to] = lit + lit * jnp.tanh(half_gain[c] * centre + half_bias[c])
        fields[3, plane - 1, to] = opacity

    inside = jnp.where(h < towers - 1, 1.0, 0.0)

    def early(plane, _):
        for row, count in spans(LEAD, rows - LEAD, 16):
            shade(plane, row, count, None)
        return 0

    lax.fori_loop(2, planes, early, 0)

    def landed(index):
        step_d, step_h = routes[index][0]
        ok, source = near(-step_d, -step_h)

        @pl.when(ok)
        def _():
            halo(index, source).wait_recv()

    def shade_low():
        for index in (0, 1, 2):
            landed(index)
        for plane in range(1, planes + 1):
            shade(plane, 0, LEAD, None)
        for row, count in spans(LEAD, rows - LEAD, 16):
            for plane in (1, planes):
                shade(plane, row, count, None)

    def shade_high():
        for index in (3, 4, 5):
            landed(index)

        def bottom(at, _):
            for plane in (2 * at + 1, 2 * at + 2):
                shade(plane, rows - LEAD, LEAD, None)
                for row, count in spans(rows, rows + margin, 16):
                    shade(plane, row, count, inside)
            return 0

        lax.fori_loop(0, planes // 2, bottom, 0)

    first_plane = d * planes

    def partial(view, block):
        step = shear[view]
        backward = reverse[view]
        colour = [jnp.zeros((share, cols), jnp.float32) for _ in range(3)]
        clear = jnp.ones((share, cols), jnp.float32)
        covered = jnp.zeros((share, cols), jnp.float32)
        for i in range(planes):
            plane = i + backward * (planes - 1 - 2 * i)
            offset = lax.div((first_plane + plane) * step, jnp.int32(total_planes))
            at = pl.ds(offset + block * share, share)
            for c in range(3):
                colour[c] = colour[c] + clear * fields[c, plane, at]
            covered = covered + clear * fields[3, plane, at]
            clear = 1.0 - covered
        return colour + [covered]

    odd = lax.rem(d, 2)
    out_step = 2 * odd - 1
    mate = d - out_step
    pair = lax.div(d, 2)
    beyond = odd * (groups - 1 - d) + (1 - odd) * d
    handing = odd * (d - 1) + (1 - odd) * (groups - 2 - d)

    def over(first, second, swap):
        front = [jnp.where(swap, b, a) for a, b in zip(first, second)]
        behind = [jnp.where(swap, a, b) for a, b in zip(first, second)]
        clear = 1.0 - front[3]
        return [f + clear * b for f, b in zip(front, behind)]

    def load(ref, block, view):
        return [ref[block, view, c] for c in range(4)]

    def store(ref, block, view, image):
        for c in range(4):
            ref[block, view, c] = image[c]

    def hand(view, block):
        return pltpu.make_async_remote_copy(
            src_ref=outgoing.at[block, view],
            dst_ref=handed.at[block, view],
            send_sem=hand_send.at[view, block],
            recv_sem=hand_recv.at[view, block],
            device_id=(mate, h),
            device_id_type=MESH,
        )

    def send(view, block):
        return pltpu.make_async_remote_copy(
            src_ref=outgoing.at[block, view],
            dst_ref=incoming.at[d, view],
            send_sem=part_send.at[view, block],
            recv_sem=part_recv.at[view, d],
            device_id=(block, h),
            device_id_type=MESH,
        )

    def receive(view, source):
        return pltpu.make_async_remote_copy(
            src_ref=outgoing.at[source, view],
            dst_ref=incoming.at[source, view],
            send_sem=part_send.at[view, source],
            recv_sem=part_recv.at[view, source],
            device_id=(source, h),
            device_id_type=MESH,
        )

    def each(count, body):
        def step(k, _):
            body(k)
            return 0

        lax.fori_loop(0, count, step, 0)

    def hand_over(view, k):
        block = odd * k + (1 - odd) * (groups - 1 - k)
        store(outgoing, block, view, partial(view, block))
        hand(view, block).start()

    def prepare(view, k):
        block = d + out_step * (1 + k)
        store(outgoing, block, view, partial(view, block))

    def to_mate(view):
        store(outgoing, mate, view, partial(view, mate))
        send(view, mate).start()

    def pass_on(view, k):
        block = odd * (groups - 1 - k) + (1 - odd) * k
        hand(view, block).wait_recv()
        own_part, other = load(outgoing, block, view), load(handed, block, view)
        swap = reverse[view] != odd
        store(outgoing, block, view, over(own_part, other, swap))
        send(view, block).start()

    reach = lax.div((first_plane + planes - 1) * margin, jnp.int32(total_planes))

    def hand_round(early):
        def one(k):
            block = odd * k + (1 - odd) * (groups - 1 - k)
            ready = ((block + 1) * share + reach <= rows - LEAD) & (odd == 1)

            @pl.when(ready if early else jnp.logical_not(ready))
            def _():
                each(views, lambda view: hand_over(view, k))

        each(handing, one)

    shade_low()
    hand_round(True)
    shade_high()
    hand_round(False)
    each(views, to_mate)
    each(views, lambda view: each(beyond, lambda k: prepare(view, k)))
    each(views, lambda view: store(incoming, d, view, partial(view, d)))
    each(beyond, lambda k: each(views, lambda view: pass_on(view, k)))

    def finish(view):
        swap = reverse[view] == 1
        receive(view, mate).wait_recv()
        both = over(load(incoming, d, view), load(incoming, mate, view), reverse[view] != odd)
        store(incoming, 2 * pair + 1, view, both)
        sources = [jnp.where(j > pair, 2 * j, 2 * j + 1) for j in range(groups // 2)]
        for j, source in enumerate(sources):

            @pl.when(j != pair)
            def _():
                receive(view, source).wait_recv()

        total = load(incoming, sources[0], view)
        for source in sources[1:]:
            total = over(total, load(incoming, source, view), swap)
        for c in range(4):
            out[c, view] = total[c]

    for view in range(views):
        finish(view)

    for index, route in enumerate(routes):
        ok, target = near(*route[0])

        @pl.when(ok)
        def _(index=index, target=target):
            halo(index, target).wait_send()

    def sent(view):
        send(view, mate).wait_send()
        each(handing, lambda k: hand(view, d - out_step * (2 + k)).wait_send())
        each(beyond, lambda k: send(view, d + out_step * (1 + k)).wait_send())

    each(views, sent)


def on_device(groups, towers, density, light, gain, bias, shear, reverse):
    planes, rows, cols = density.shape
    views = shear.shape[0]
    share = rows // groups
    tall = LEAD + rows + rows // 2
    scalars = pl.BlockSpec(memory_space=pltpu.SMEM)
    return pl.pallas_call(
        functools.partial(kernel, groups, towers),
        name="render",
        out_shape=pltpu.VMEM((4, views, share, cols), jnp.float32),
        in_specs=[pl.BlockSpec(memory_space=pltpu.HBM)] + [scalars] * 5,
        out_specs=pl.BlockSpec(memory_space=pltpu.VMEM),
        scratch_shapes=[
            pltpu.VMEM((planes + 2, tall + LEAD, cols), jnp.float32),
            pltpu.VMEM((4, planes, rows + rows // 2, cols), jnp.float32),
            pltpu.VMEM((groups, views, 4, share, cols), jnp.float32),
            pltpu.VMEM((groups, views, 4, share, cols), jnp.float32),
            pltpu.VMEM((groups, views, 4, share, cols), jnp.float32),
            pltpu.SemaphoreType.DMA,
            pltpu.SemaphoreType.DMA((6,)),
            pltpu.SemaphoreType.DMA((6,)),
            pltpu.SemaphoreType.DMA((views, groups)),
            pltpu.SemaphoreType.DMA((views, groups)),
            pltpu.SemaphoreType.DMA((views, groups)),
            pltpu.SemaphoreType.DMA((views, groups)),
        ],
        compiler_params=pltpu.CompilerParams(collective_id=0, has_side_effects=True, vmem_limit_bytes=60 * 1024 * 1024),
    )(density, light, gain, bias, shear, reverse)


def solution(mesh):
    groups, towers = mesh.shape["depth"], mesh.shape["height"]
    placed = (P("depth", "height", None), P(), P(), P(), P(), P())
    return jax.shard_map(
        functools.partial(on_device, groups, towers),
        mesh=mesh,
        in_specs=placed,
        out_specs=P(None, None, ("height", "depth"), None),
        check_vma=False,
    )
```
